256 devices in a mesh: depth: 32 (over x, z_hi, core), filt: 8 (over z_lo, y).
Axes of the slice: x: 4, y: 4, z: 8 (z_hi: 4, z_lo: 2; z = z_hi * 2 + z_lo), core: 2. Of those that a mesh axis runs over, the one named last changes fastest.
Arguments:
- volume: bfloat16 [256, 32, 4096], P('filt', 'depth'), may hold values from -6 to 6
- kernel: bfloat16 [27, 256, 256], P(None, 'filt'), may hold values from -0.078125 to 0.078125
- bias: float32 [256], P('filt'), may hold values from -3 to 3
- cotangent: bfloat16 [256, 32, 4096], P('filt', 'depth'), may hold values from -6 to 6
Outputs:
- activated: bfloat16 [256, 32, 4096], P('filt', 'depth')
- input_grad: bfloat16 [256, 32, 4096], P('filt', 'depth')
- kernel_grad: float32 [27, 256, 256], P(None, 'filt')
- bias_grad: float32 [256], P('filt')
The draws below stay inside these ranges and needn't reach their ends.
All inputs are finite; a program needn't handle non-finite values.
Results may differ from the reference program's by a relative error of at most 0.0055.
Values may be sent and summed in bfloat16 or wider, within the bound.
No kernel may reach another device: no remote copies, remote signals or barrier semaphores. Data moves between devices by JAX's collectives and lax.ppermute only.
A program may use at most 64 MiB of HBM per device.

```python
import jax
import jax.numpy as jnp
from jax import lax

CH = 256
HEIGHT = 64
WIDTH = 64
DEPTH = 32


def steps_of(rng, shape, cuts, low, top_value):
    gain = 1.0
    for axis_at, shards_of in cuts:
        heights = jax.random.uniform(jax.random.fold_in(jax.random.fold_in(rng, 6), axis_at), (shards_of,), jnp.float32, low / len(cuts), top_value / len(cuts))
        gain = gain * jnp.repeat(jnp.exp(heights), shape[axis_at] // shards_of).reshape((-1,) + (1,) * (len(shape) - 1 - axis_at))
    return gain


def bell_draw(key, extent, width, most, cuts=(), kind=jnp.bfloat16):
    result = jax.random.normal(key, extent, jnp.float32) * width
    if len(cuts) > 0:
        result = steps_of(key, extent, cuts, -0.22, 0.18) * result
    return jnp.clip(result, min=-most, max=most).astype(kind)


def setup_inputs(seed: int = 0) -> dict:
    arg_keys = jax.random.split(jax.random.key(seed), 5)
    return {
        "volume": bell_draw(arg_keys[0], (CH, DEPTH, HEIGHT * WIDTH), 1.0, 6.0, ((0, 8), (1, 32))),
        "kernel": bell_draw(arg_keys[1], (27, CH, CH), (27 * CH) ** -0.5, 0.078125, ((1, 8),)),
        "bias": bell_draw(arg_keys[2], (CH,), 0.5, 3.0, ((0, 8),), jnp.float32),
        "cotangent": bell_draw(arg_keys[3], (CH, DEPTH, HEIGHT * WIDTH), 1.0, 6.0, ((0, 8), (1, 32))),
    }


def shift_out(values, down_by, right_by):
    length = values.shape[-1]
    offset = down_by * WIDTH + right_by
    if offset > 0:
        filler = jnp.zeros(values.shape[:-1] + (offset,), values.dtype)
        moved = jnp.concatenate([values[..., offset:], filler], axis=-1)
    elif offset < 0:
        filler = jnp.zeros(values.shape[:-1] + (-offset,), values.dtype)
        moved = jnp.concatenate([filler, values[..., :length + offset]], axis=-1)
    else:
        moved = values
    column = jnp.arange(length, dtype=jnp.int32) % WIDTH
    inside = (column + right_by >= 0) & (column + right_by < WIDTH)
    return jnp.where(inside, moved, jnp.zeros((), values.dtype))

def smooth_gate(values):
    return jax.nn.gelu(values, approximate=True)

def reference(volume, kernel, bias, cotangent):
    planes_all = volume.shape[1]
    padded = jnp.pad(volume, ((0, 0), (1, 1), (0, 0))).astype(jnp.float32)
    taps = kernel.astype(jnp.float32)
    preact = jnp.zeros(volume.shape, jnp.float32) + bias[:, None, None]
    for depth_tap in range(3):
        planes = padded[:, depth_tap:depth_tap + planes_all]
        for plane_tap in range(9):
            index = 9 * depth_tap + plane_tap
            products = jnp.einsum('oc,cdp->odp', taps[index], planes)
            preact = preact + shift_out(products, plane_tap // 3 - 1, plane_tap % 3 - 1)
    activation, pullback = jax.vjp(smooth_gate, preact)
    activated = activation.astype(jnp.bfloat16)
    grad_pre = pullback(cotangent.astype(jnp.float32))[0].astype(jnp.bfloat16)
    grad_float = grad_pre.astype(jnp.float32)
    bias_grad = lax.optimization_barrier(jnp.sum(grad_float, axis=(1, 2)))
    grad_padded = jnp.pad(grad_float, ((0, 0), (1, 1), (0, 0)))
    summed = jnp.zeros(volume.shape, jnp.float32)
    pieces = []
    for depth_tap in range(3):
        grad_planes = grad_padded[:, 2 - depth_tap:2 - depth_tap + planes_all]
        planes = padded[:, depth_tap:depth_tap + planes_all]
        for plane_tap in range(9):
            index = 9 * depth_tap + plane_tap
            down_by = 1 - plane_tap // 3
            right_by = 1 - plane_tap % 3
            products = jnp.einsum('oc,odp->cdp', taps[index], grad_planes)
            summed = summed + shift_out(products, down_by, right_by)
            shifted = shift_out(grad_float, down_by, right_by)
            pieces.append(jnp.einsum('odp,cdp->oc', shifted, planes))
    kernel_grad = jnp.stack(pieces, axis=0)
    return (activated, summed.astype(jnp.bfloat16), kernel_grad, bias_grad)
```

```python
import functools

import jax
import jax.numpy as jnp
from jax import lax
from jax.experimental import pallas as pl
from jax.experimental.pallas import tpu as pltpu
from jax.sharding import PartitionSpec as P


BF = jnp.bfloat16
F32 = jnp.float32
ROW = 64
OWN = 32 * ROW
GWIN = 34 * ROW
VWIN = 36 * ROW
VMEM = pl.BlockSpec(memory_space=pltpu.VMEM)
SMEM = pl.BlockSpec(memory_space=pltpu.SMEM)
SHIFTS = (1, 3, 2)


def filt_pairs(dy, dz):
    return [(z * 4 + y, (z ^ dz) * 4 + (y + dy) % 4) for z in range(2) for y in range(4)]


def depth_pairs(dx, dh, dc):
    return [
        ((x * 4 + h) * 2 + c, ((x + dx) % 4 * 4 + (h + dh) % 4) * 2 + (c ^ dc))
        for x in range(4)
        for h in range(4)
        for c in range(2)
    ]


def call(body, outs, scratch, *args, flops=0, moved=4_000_000):
    return pl.pallas_call(
        body,
        out_shape=outs,
        in_specs=[SMEM] + [VMEM] * (len(args) - 1),
        out_specs=jax.tree.map(lambda _: VMEM, outs),
        scratch_shapes=scratch,
        compiler_params=pltpu.CompilerParams(vmem_limit_bytes=48 * 1024 * 1024),
        cost_estimate=pl.CostEstimate(flops=flops, bytes_accessed=moved, transcendentals=0),
    )(*args)


def column(shape):
    return lax.broadcasted_iota(jnp.int32, shape, 1) % ROW


def shifted_columns(values, by):
    if by == 0:
        return values
    moved = pltpu.roll(values, (-by) % values.shape[1], 1)
    at = column(values.shape)
    inside = at < ROW - 1 if by > 0 else at > 0
    return jnp.where(inside, moved, jnp.zeros_like(moved))


def forward_body(place, *refs):
    shards, weights = refs[:8], refs[8]
    low, mid, high, own = refs[9:13]
    window, stack = refs[13:]
    z, y = place[0], place[1]
    window[:, pl.ds(pl.multiple_of(GWIN * z, 128), 128)] = jnp.zeros((256, 128), BF)
    at = pl.multiple_of(128 * (1 - z), 128)
    sources = [(0, 0), (0, 1)] + [(s, dz) for dz in range(2) for s in SHIFTS]
    for (s, dz), shard in zip(sources, shards, strict=True):
        block = ((z + dz) % 2) * 4 + (y + 4 - s) % 4
        window[pl.ds(pl.multiple_of(block * 32, 32), 32), pl.ds(at, GWIN)] = shard[...]
    own[...] = window[:, 2 * ROW : 2 * ROW + OWN]

    def build(i, _):
        rows = pl.ds(pl.multiple_of(i * 32, 32), 32)
        values = window[rows, :]
        for c in range(3):
            moved = shifted_columns(values.astype(F32), c - 1).astype(BF)
            for b in range(3):
                k = pl.multiple_of((b * 3 + c) * 256 + i * 32, 32)
                stack[pl.ds(k, 32), :] = moved[:, ROW * b : ROW * b + GWIN]
        return 0

    lax.fori_loop(0, 8, build, 0)
    for n in range(0, GWIN, 256):
        cells = slice(n, min(n + 256, GWIN))
        got = jnp.dot(weights[...], stack[:, cells], preferred_element_type=F32)
        low[:, cells] = got[:64].astype(BF)
        mid[:, cells] = got[64:128]
        high[:, cells] = got[128:].astype(BF)


def gelu_body(place, mid, below, above, bias, cot_own, cot_other, act_own, act_other, grad, sums, cot):
    z = place[0]
    mine, other = pl.multiple_of(z * 32, 32), pl.multiple_of((1 - z) * 32, 32)
    cot[pl.ds(mine, 32), :] = cot_own[...]
    cot[pl.ds(other, 32), :] = cot_other[...]
    v = mid[...] + bias[...] + below[...].astype(F32) + above[...].astype(F32)
    root = 0.7978845608028654
    square = v * v
    t = jnp.tanh(root * (v + 0.044715 * (square * v)))
    half = 0.5 * (1.0 + t)
    slope = half + 0.5 * v * (1.0 - t * t) * (root * (1.0 + 3 * 0.044715 * square))
    g = (cot[...].astype(F32) * slope).astype(BF)
    grad[...] = g
    act = (v * half)[:, ROW : ROW + OWN]
    sums[...] = jnp.sum(g.astype(F32)[:, ROW : ROW + OWN], axis=1, keepdims=True)
    lower = z == 0
    act_own[...] = jnp.where(lower, act[:32], act[32:]).astype(BF)
    act_other[...] = jnp.where(lower, act[32:], act[:32]).astype(BF)


def shifted_grads(grads, stack):
    for a in range(3):
        values = grads[2 - a][...].astype(F32)
        for c in range(3):
            moved = shifted_columns(values, 1 - c).astype(BF)
            for b in range(3):
                k = (9 * a + 3 * b + c) * 64
                start = ROW * (2 - b)
                stack[k : k + 64, :] = moved[:, start : start + OWN]


def kernel_grad_body(place, below, here, above, own, sums, keep, send, stack):
    shifted_grads((below, here, above), stack)
    core = place[2]
    for m in range(0, 28 * 64, 256):
        rows = slice(m, min(m + 256, 27 * 64))
        got = lax.dot_general(
            stack[rows, :], own[...], (((1,), (1,)), ((), ())), preferred_element_type=F32
        )
        left, right = got[:, :128], got[:, 128:]
        keep[rows, :] = jnp.where(core == 0, left, right)
        send[rows, :] = jnp.where(core == 0, right, left)
    spread = jnp.broadcast_to(sums[...], (64, 128))
    keep[27 * 64 :, :] = spread
    send[27 * 64 :, :] = spread


def input_grad_body(place, below, here, above, weights, *refs):
    outs, (stack, full) = refs[:8], refs[8:]
    shifted_grads((below, here, above), stack)
    for n in range(0, OWN, 256):
        full[:, n : n + 256] = jnp.dot(
            weights[...], stack[:, n : n + 256], preferred_element_type=F32
        ).astype(BF)
    z, y = place[0], place[1]
    for (s, dz), out in zip(TARGETS, outs, strict=True):
        block = ((z + dz) % 2) * 4 + (y + s) % 4
        out[...] = full[pl.ds(pl.multiple_of(block * 32, 32), 32), :]


TARGETS = tuple((s, dz) for dz in range(2) for s in (0,) + SHIFTS)


def total_body(place, *refs):
    parts, out = refs[:8], refs[8]
    z = place[0]
    for dz in range(2):
        four = [p[...].astype(F32) for p in parts[4 * dz : 4 * dz + 4]]
        at = pl.multiple_of(((z + dz) % 2) * OWN, 128)
        out[:, pl.ds(at, OWN)] = ((four[0] + four[3]) + (four[1] + four[2])).astype(BF)


def shape(dims, dtype):
    return jax.ShapeDtypeStruct(dims, dtype)


def pick(first, a, b, axis):
    return jnp.where(first, jnp.concatenate([a, b], axis), jnp.concatenate([b, a], axis))


def local(volume, kernel, bias, cotangent):
    filt, depth = lax.axis_index("filt"), lax.axis_index("depth")
    z, y = filt // 4, filt % 4
    x, core = depth // 8, depth % 2
    place = jnp.stack([z, y, core, x]).astype(jnp.int32)

    def across(value, dy, dz):
        return lax.ppermute(value, "filt", filt_pairs(dy, dz))

    def along(value, dx, dh, dc):
        return lax.ppermute(value, "depth", depth_pairs(dx, dh, dc))

    flat = volume.reshape(32, 64 * ROW)
    half = lambda which: lax.dynamic_slice(flat, (0, which * (30 * ROW)), (32, GWIN))
    mine = half(z)
    partner = across(half(1 - z), 0, 1)
    shards = [mine, partner]
    shards += [across(mine, s, 0) for s in SHIFTS]
    shards += [across(partner, s, 0) for s in SHIFTS]

    taps = lax.dynamic_slice(kernel, (0, 0, 128 * core), (27, 32, 128))
    taps = across(taps, 0, 1)
    taps = pick(core == 0, taps, along(taps, 0, 0, 1), 2)
    filters = pick(z == 0, kernel, taps, 1)
    forward_weights = filters.reshape(3, 9, 64, 256).transpose(0, 2, 1, 3).reshape(192, 9 * 256)
    backward_weights = filters.reshape(27 * 64, 256).T
    biases = pick(z == 0, bias, across(bias, 0, 1), 0).reshape(64, 1)
    padded = jnp.pad(cotangent.reshape(32, 64 * ROW), ((0, 0), (ROW, ROW)))
    half_cot = lambda which: lax.dynamic_slice(padded, (0, which * OWN), (32, GWIN))
    cot_own = half_cot(z)
    cot_other = across(half_cot(1 - z), 0, 1)

    up = [(i, i + 1) for i in range(31)]
    down = [(i + 1, i) for i in range(31)]
    low, mid, high, own = call(
        forward_body,
        (shape((64, GWIN), BF), shape((64, GWIN), F32), shape((64, GWIN), BF), shape((256, OWN), BF)),
        [pltpu.VMEM((256, VWIN), BF), pltpu.VMEM((9 * 256, GWIN), BF)],
        place,
        *shards,
        forward_weights,
        flops=2 * 192 * 2304 * GWIN,
    )
    below = lax.ppermute(low, "depth", up)
    above = lax.ppermute(high, "depth", down)
    act_own, act_other, grad, sums = call(
        gelu_body,
        (shape((32, OWN), BF), shape((32, OWN), BF), shape((64, GWIN), BF), shape((64, 1), F32)),
        [pltpu.VMEM((64, GWIN), BF)],
        place,
        mid,
        below,
        above,
        biases,
        cot_own,
        cot_other,
    )
    grad_below = lax.ppermute(grad, "depth", up)
    grad_above = lax.ppermute(grad, "depth", down)
    activated = pick(z == 0, act_own, across(act_other, 0, 1), 1)

    stack = pltpu.VMEM((27 * 64, OWN), BF)
    keep, send = call(
        kernel_grad_body,
        (shape((28 * 64, 128), F32), shape((28 * 64, 128), F32)),
        [stack],
        place,
        grad_below,
        grad,
        grad_above,
        own,
        sums,
        flops=2 * 1728 * 256 * OWN,
    )
    pieces = call(
        input_grad_body,
        tuple(shape((32, OWN), BF) for _ in range(8)),
        [stack, pltpu.VMEM((256, OWN), BF)],
        place,
        grad_below,
        grad,
        grad_above,
        backward_weights,
        flops=2 * 1728 * 256 * OWN,
    )

    part = (keep + along(send, 0, 0, 1)).reshape(28, 2, 4, 8, 128)
    quarter = lambda which: lax.dynamic_slice_in_dim(part, which % 4, 1, 2)[:, :, 0]
    got = [along(quarter(x + s).astype(BF), s, 0, 0).astype(F32) for s in SHIFTS]
    part = quarter(x) + got[0] + got[1] + got[2]
    side = lambda which: lax.dynamic_slice_in_dim(part, which, 1, 1)[:, 0]
    part = (side(z) + across(side(1 - z), 0, 1)).astype(BF)
    got = [along(part, 0, s, 0).astype(F32) for s in SHIFTS]
    part = (part.astype(F32) + got[2]) + (got[0] + got[1])
    got = {s: along(part, s, 0, 0) for s in SHIFTS}
    ring = jnp.stack([part, got[3], got[2], got[1]] * 2)
    ring = lax.dynamic_slice_in_dim(ring, (4 - x) % 4, 4, 0)
    part = ring.transpose(1, 0, 2, 3).reshape(28, 32, 128)
    whole = pick(core == 0, part, along(part, 0, 0, 1), 2)
    kernel_grad, bias_grad = whole[:27], whole[27, :, 0]

    parts = [
        piece if (s, dz) == (0, 0) else across(piece, s, dz)
        for (s, dz), piece in zip(TARGETS, pieces, strict=True)
    ]
    input_grad = call(total_body, shape((32, 64 * ROW), BF), [], place, *parts)
    return (
        activated.reshape(32, 1, 64 * ROW),
        input_grad.reshape(32, 1, 64 * ROW),
        kernel_grad,
        bias_grad,
    )


def solution(mesh):
    placed = (P("filt", "depth", None), P(None, "filt", None), P("filt"), P("filt", "depth", None))
    return jax.shard_map(
        local,
        mesh=mesh,
        in_specs=placed,
        out_specs=(
            P("filt", "depth", None),
            P("filt", "depth", None),
            P(None, "filt", None),
            P("filt"),
        ),
        check_vma=False,
    )
```

```python
import jax
import jax.numpy as jnp
from jax import lax
from jax.experimental import pallas as pl
from jax.experimental.pallas import tpu as pltpu
from jax.sharding import PartitionSpec as P


BF = jnp.bfloat16
F32 = jnp.float32
ROW = 64
OWN = 32 * ROW
GWIN = 34 * ROW
VWIN = 36 * ROW
VMEM = pl.BlockSpec(memory_space=pltpu.VMEM)
SMEM = pl.BlockSpec(memory_space=pltpu.SMEM)
HBM = pl.BlockSpec(memory_space=pltpu.HBM)
PEERS = (1, 3, 2)
STEPS = (0,) + PEERS


def peer(index, s):
    return 3 - index if s == 3 else index ^ s


def pairs(move):
    found = []
    for i in range(256):
        x, h, c, z, y = i // 64, i // 16 % 4, i // 8 % 2, i // 4 % 2, i % 4
        to = move(x, h, c, z, y)
        if to is not None:
            x, h, c, z, y = to
            found.append((i, (((x % 4) * 4 + h % 4) * 2 + c % 2) * 8 + z % 2 * 4 + y % 4))
    return found


def far_plane(x, h, c, z, y):
    plane = x * 8 + h * 2 + z + (1 if z else -1)
    return (plane // 8, plane // 2 % 4, c, plane % 2, y) if 0 <= plane < 32 else None


def straight(x, h, c, z, y):
    return x, h, z, c, y


def crossed_in(x, h, c, z, y):
    return x, h, 1 - z, c, y


def crossed_out(x, h, c, z, y):
    return x, h, z, 1 - c, y


def other_core(x, h, c, z, y):
    return x, h, 1 - c, z, y


def other_z(x, h, c, z, y):
    return x, h, c, 1 - z, y


def pair_h(x, h, c, z, y):
    return x, h ^ 1, c, z, y


def mirror_h(x, h, c, z, y):
    return x, 3 - h, c, z, y


def pair_zh(x, h, c, z, y):
    return x, h ^ 1, c, 1 - z, y


def peer_x(s):
    return lambda x, h, c, z, y: (peer(x, s), h, c, z, y)


def peer_y(s):
    return lambda x, h, c, z, y: (x, h, c, z, peer(y, s))


def exchange(value, move):
    return lax.ppermute(value, ("depth", "filt"), pairs(move))


def shape(*dims, dtype=BF):
    return jax.ShapeDtypeStruct(dims, dtype)


def call(body, outs, scratch, *args, flops=0, moved=2_000_000, room=4, hbm_in=(), hbm_out=()):
    return pl.pallas_call(
        body,
        out_shape=outs,
        in_specs=[SMEM] + [HBM if i in hbm_in else VMEM for i in range(1, len(args))],
        out_specs=tuple(HBM if i in hbm_out else VMEM for i in range(len(outs))),
        scratch_shapes=scratch,
        compiler_params=pltpu.CompilerParams(vmem_limit_bytes=room * 1024 * 1024),
        cost_estimate=pl.CostEstimate(flops=flops, bytes_accessed=moved, transcendentals=0),
    )(*args)


def at(index, size):
    return pl.ds(pl.multiple_of(index * size, size), size)


Z, Y, C, X = range(4)


def shifted_columns(values, by):
    if by == 0:
        return values
    moved = pltpu.roll(values, (-by) % values.shape[1], 1)
    column = lax.broadcasted_iota(jnp.int32, values.shape, 1) % ROW
    inside = column < ROW - 1 if by > 0 else column > 0
    return jnp.where(inside, moved, jnp.zeros_like(moved))


def prepare_body(place, mine, partner, partner_rest, forward, backward, filters):
    z, c = place[Z], place[C]
    for k in range(27):
        filters[k, at(z, 32), :] = mine[k]
        filters[k, at(1 - z, 32), at(c, 128)] = partner[k]
        filters[k, at(1 - z, 32), at(1 - c, 128)] = partner_rest[k]
    for k in range(27):
        a, b, d = k // 9, k // 3 % 3, k % 3
        row = (d * 3 + a) * 64
        forward[row : row + 64, 256 * b : 256 * b + 256] = filters[k]
    for k in range(0, 27, 2):
        two = filters[k : min(k + 2, 27)].reshape(-1, 256)
        backward[:, 64 * k : 64 * k + two.shape[0]] = two.T


def forward_body(place, *refs):
    shards, weights = refs[:4], refs[4]
    near, mid, far, own = refs[5:9]
    window, moved, sem = refs[9:]
    y, c = place[Y], place[C]
    window[:, pl.ds(pl.multiple_of(GWIN * c, 128), 128)] = jnp.zeros((256, 128), BF)
    start = pl.ds(pl.multiple_of(128 * (1 - c), 128), GWIN)
    for s, shard in zip(STEPS, shards, strict=True):
        for i in range(2):
            block = (c + i) % 2 * 4 + peer(y, s)
            window[at(block, 32), start] = shard[32 * i : 32 * i + 32, :]
    keep = pltpu.make_async_copy(window.at[:, 2 * ROW : 2 * ROW + OWN], own, sem)
    keep.start()

    def build(i, _):
        moved[at(i, 32), :] = window[at(i, 32), :][:, ROW : ROW + GWIN]
        return 0

    lax.fori_loop(0, 8, build, 0)
    for n in range(0, GWIN, 256):
        size = min(256, GWIN - n)
        planes = (window[:, n : n + size], moved[:, n : n + size], window[:, n + 128 : n + 128 + size])
        got = jnp.dot(weights[...], jnp.concatenate(planes), preferred_element_type=F32)
        total = shifted_columns(got[:192], -1) + got[192:384] + shifted_columns(got[384:], 1)
        cells = slice(n, n + size)
        to_next, to_last = total[:64].astype(BF), total[128:].astype(BF)
        near[:, cells] = jnp.where(place[Z] == 0, to_next, to_last)
        mid[:, cells] = total[64:128]
        far[:, cells] = jnp.where(place[Z] == 0, to_last, to_next)
    keep.wait()


def gelu_parts(mid, near, far, bias):
    v = mid[...] + bias[...] + near[...].astype(F32) + far[...].astype(F32)
    square = v * v
    t = jnp.tanh(0.7978845608028654 * (v + 0.044715 * (square * v)))
    return v, square, t


def grad_body(place, mid, near, far, bias, cot_own, cot_other, grad, sums, cot):
    c = place[C]
    cot[at(c, 32), :] = cot_own[...]
    cot[at(1 - c, 32), :] = cot_other[...]
    v, square, t = gelu_parts(mid, near, far, bias)
    inner = 0.7978845608028654 * (1.0 + 3 * 0.044715 * square)
    slope = 0.5 * (1.0 + t) + 0.5 * v * (1.0 - t * t) * inner
    g = (cot[...].astype(F32) * slope).astype(BF)
    grad[...] = g
    sums[...] = jnp.sum(g.astype(F32)[:, ROW : ROW + OWN], axis=1, keepdims=True)


def activated_body(place, mid, near, far, bias, mine, other, act):
    v, _, t = gelu_parts(mid, near, far, bias)
    act[...] = (v * (0.5 * (1.0 + t)))[:, ROW : ROW + OWN].astype(BF)
    mine[...] = act[at(place[C], 32), :]
    other[...] = act[at(1 - place[C], 32), :]


def shifted_grads(place, near, here, far, stack):
    lower = place[Z] == 0
    above, below = jnp.where(lower, near[...], far[...]), jnp.where(lower, far[...], near[...])
    for a, values in enumerate((above, here[...], below)):
        values = values.astype(F32)
        for c in range(3):
            moved = shifted_columns(values, 1 - c).astype(BF)
            for b in range(3):
                k = (9 * a + 3 * b + c) * 64
                start = ROW * (2 - b)
                stack[k : k + 64, :] = moved[:, start : start + OWN]


def split(values, out):
    high = values.astype(BF)
    out[...] = high
    n = values.shape[0] * 27 // 28
    low = (values[n:] - high[n:].astype(F32)).astype(BF)
    lane = lax.broadcasted_iota(jnp.int32, low.shape, 2)
    out[n:] = jnp.where(lane < 64, high[n:], low)


def join(ref):
    values = ref[...].astype(F32)
    n = values.shape[0] * 27 // 28
    last = values[n:]
    return jnp.concatenate([values[:n], last + pltpu.roll(last, 64, 2)])


def kernel_grad_body(place, near, here, far, own, sums, keep, send, stack, volume, sem):
    fetch = pltpu.make_async_copy(own, volume, sem)
    fetch.start()
    shifted_grads(place, near, here, far, stack)
    fetch.wait()
    core = place[C]
    for m in range(0, 27, 4):
        n = min(4, 27 - m)
        got = lax.dot_general(
            stack[64 * m : 64 * (m + n), :],
            volume[...],
            (((1,), (1,)), ((), ())),
            preferred_element_type=F32,
        )
        left, right = got[:, :128], got[:, 128:]
        taps = slice(2 * m, 2 * (m + n))
        keep[taps] = jnp.where(core == 0, left, right).reshape(2 * n, 32, 128)
        send[taps] = jnp.where(core == 0, right, left).reshape(2 * n, 32, 128).astype(BF)
    spread = jnp.broadcast_to(sums[...], (64, 128))
    keep[54:] = spread.reshape(2, 32, 128)
    split_last = spread.astype(BF)
    rest = (spread - split_last.astype(F32)).astype(BF)
    lane = lax.broadcasted_iota(jnp.int32, rest.shape, 1)
    send[54:] = jnp.where(lane < 64, split_last, rest).reshape(2, 32, 128)


def input_grad_body(place, near, here, far, weights, *refs):
    outs, (stack, full) = refs[:4], refs[4:]
    shifted_grads(place, near, here, far, stack)
    for n in range(0, OWN, 256):
        full[:, n : n + 256] = jnp.dot(
            weights[...], stack[:, n : n + 256], preferred_element_type=F32
        ).astype(BF)
    y, c = place[Y], place[C]
    for s, out in zip(STEPS, outs, strict=True):
        for i in range(2):
            block = (c + i) % 2 * 4 + peer(y, s)
            out[32 * i : 32 * i + 32, :] = full[at(block, 32), :]


def fold_y_body(place, one, two, three, four, act_own, act_other, straight_out, crossed_out):
    total = (one[...].astype(F32) + four[...].astype(F32)) + (two[...].astype(F32) + three[...].astype(F32))
    total = total.astype(BF)
    straight_out[:32, :] = act_own[...]
    crossed_out[:32, :] = act_other[...]
    straight_out[32:, :] = total[:32]
    crossed_out[32:, :] = total[32:]


def place_body(place, direct, crossed, activated, input_grad):
    z = place[Z]
    for part, half in ((direct, z), (crossed, 1 - z)):
        activated[:, at(half, OWN)] = part[:32, :]
        input_grad[:, at(half, OWN)] = part[32:, :]


def fold_core_body(place, keep, got, mine, *refs):
    outs, total = refs[:3], refs[3]
    total[...] = keep[...] + join(got)
    x = place[X]
    mine[...] = total[:, at(x, 8), :]
    for s, out in zip(PEERS, outs, strict=True):
        split(total[:, at(peer(x, s), 8), :], out)


def fold_x_body(place, mine, one, two, three, keep, send, total):
    total[...] = (mine[...] + join(one) + join(two) + join(three)).reshape(28, 2, 8, 128)
    split(total[:, pl.ds(place[Z], 1)].reshape(28, 8, 128), keep)
    split(total[:, pl.ds(1 - place[Z], 1)].reshape(28, 8, 128), send)


def fold_zh_body(place, mine, from_z, from_h, from_zh, out):
    split((join(mine) + join(from_z)) + (join(from_h) + join(from_zh)), out)


def fold_h_body(place, mine, got, out):
    split(join(mine) + join(got), out)


def quarters_body(place, *refs):
    parts, out, full = refs[:4], refs[4], refs[5]
    for s, part in zip(STEPS, parts, strict=True):
        full[:, at(peer(place[X], s), 8), :] = part[...].astype(F32)
    out[...] = full[...].astype(BF)


def whole_body(place, mine, other, taps, bias):
    taps[:, :, at(place[C], 128)] = mine[:27].astype(F32)
    taps[:, :, at(1 - place[C], 128)] = other[:27].astype(F32)
    last = mine[27].astype(F32)
    bias[...] = (last + pltpu.roll(last, 64, 1)).T[:1]


def local(volume, kernel, bias, cotangent):
    filt, depth = lax.axis_index("filt"), lax.axis_index("depth")
    z, c = filt // 4, depth % 2
    place = jnp.stack([z, filt % 4, c, depth // 8]).astype(jnp.int32)

    flat = volume.reshape(32, 64 * ROW)
    first, second = flat[:, :GWIN], flat[:, 30 * ROW :]
    direct = exchange(jnp.where(z == 0, first, second), straight)
    crossed = exchange(jnp.where(z == 0, second, first), crossed_in)
    column = jnp.concatenate([direct, crossed])
    shards = [column] + [exchange(column, peer_y(s)) for s in PEERS]

    taps = exchange(lax.dynamic_slice(kernel, (0, 0, 128 * c), (27, 32, 128)), other_z)
    forward_weights, backward_weights = call(
        prepare_body,
        (shape(576, 768), shape(256, 1728)),
        [pltpu.VMEM((27, 64, 256), BF)],
        place,
        kernel,
        taps,
        exchange(taps, other_core),
        room=8,
    )
    partner_bias = exchange(bias, other_z)
    biases = jnp.where(
        z == 0, jnp.concatenate([bias, partner_bias]), jnp.concatenate([partner_bias, bias])
    ).reshape(64, 1)
    padded = jnp.pad(cotangent.reshape(32, 64 * ROW), ((0, 0), (ROW, ROW)))
    first, second = padded[:, :GWIN], padded[:, OWN:]
    cot_own = exchange(jnp.where(z == 0, first, second), straight)
    cot_other = exchange(jnp.where(z == 0, second, first), crossed_in)

    near, mid, far, own = call(
        forward_body,
        (shape(64, GWIN), shape(64, GWIN, dtype=F32), shape(64, GWIN), shape(256, OWN)),
        [pltpu.VMEM((256, VWIN), BF), pltpu.VMEM((256, GWIN), BF), pltpu.SemaphoreType.DMA],
        place,
        *shards,
        forward_weights,
        flops=2 * 192 * 2304 * GWIN,
        room=12,
        hbm_out=(3,),
    )
    near, far = exchange(near, other_z), exchange(far, far_plane)
    grad, sums = call(
        grad_body,
        (shape(64, GWIN), shape(64, 1, dtype=F32)),
        [pltpu.VMEM((64, GWIN), BF)],
        place,
        mid,
        near,
        far,
        biases,
        cot_own,
        cot_other,
        room=12,
    )
    grad_near, grad_far = exchange(grad, other_z), exchange(grad, far_plane)
    act_own, act_other = call(
        activated_body,
        (shape(32, OWN), shape(32, OWN)),
        [pltpu.VMEM((64, OWN), BF)],
        place,
        mid,
        near,
        far,
        biases,
        room=12,
    )

    stack = pltpu.VMEM((27 * 64, OWN), BF)
    keep, send = call(
        kernel_grad_body,
        (shape(56, 32, 128, dtype=F32), shape(56, 32, 128)),
        [stack, pltpu.VMEM((256, OWN), BF), pltpu.SemaphoreType.DMA],
        place,
        grad_near,
        grad,
        grad_far,
        own,
        sums,
        flops=2 * 1728 * 256 * OWN,
        room=20,
        hbm_in=(4,),
    )
    pieces = call(
        input_grad_body,
        tuple(shape(64, OWN) for _ in STEPS),
        [stack, pltpu.VMEM((256, OWN), BF)],
        place,
        grad_near,
        grad,
        grad_far,
        backward_weights,
        flops=2 * 1728 * 256 * OWN,
        room=20,
    )

    parts = [pieces[0]] + [exchange(p, peer_y(s)) for s, p in zip(PEERS, pieces[1:])]
    direct, crossed = call(
        fold_y_body, (shape(64, OWN), shape(64, OWN)), [], place, *parts, act_own, act_other
    )
    activated, input_grad = call(
        place_body,
        (shape(32, 64 * ROW), shape(32, 64 * ROW)),
        [],
        place,
        exchange(direct, straight),
        exchange(crossed, crossed_out),
    )

    mine, *sends = call(
        fold_core_body,
        (shape(56, 8, 128, dtype=F32),) + (shape(56, 8, 128),) * 3,
        [pltpu.VMEM((56, 32, 128), F32)],
        place,
        keep,
        exchange(send, other_core),
    )
    got = [exchange(value, peer_x(s)) for s, value in zip(PEERS, sends)]
    eight = shape(28, 8, 128)
    keep, send = call(
        fold_x_body, (eight, eight), [pltpu.VMEM((28, 2, 8, 128), F32)], place, mine, *got
    )
    got = [exchange(send, other_z), exchange(keep, pair_h), exchange(send, pair_zh)]
    (part,) = call(fold_zh_body, (eight,), [], place, keep, *got)
    (part,) = call(fold_h_body, (eight,), [], place, part, exchange(part, mirror_h))
    got = [exchange(part, peer_x(s)) for s in PEERS]
    (part,) = call(
        quarters_body, (shape(28, 32, 128),), [pltpu.VMEM((28, 32, 128), F32)], place, part, *got
    )
    kernel_grad, bias_grad = call(
        whole_body,
        (shape(27, 32, 256, dtype=F32), shape(1, 32, dtype=F32)),
        [],
        place,
        part,
        exchange(part, other_core),
    )
    return (
        activated.reshape(32, 1, 64 * ROW),
        input_grad.reshape(32, 1, 64 * ROW),
        kernel_grad,
        bias_grad.reshape(32),
    )


def solution(mesh):
    placed = (P("filt", "depth", None), P(None, "filt", None), P("filt"), P("filt", "depth", None))
    return jax.shard_map(
        local,
        mesh=mesh,
        in_specs=placed,
        out_specs=(
            P("filt", "depth", None),
            P("filt", "depth", None),
            P(None, "filt", None),
            P("filt"),
        ),
        check_vma=False,
    )
```

```python
import jax
import jax.numpy as jnp
from jax import lax
from jax.experimental import pallas as pl
from jax.experimental.pallas import tpu as pltpu
from jax.sharding import PartitionSpec as P


BF = jnp.bfloat16
F32 = jnp.float32
ROW = 64
OWN = 32 * ROW
GWIN = 34 * ROW
VWIN = 36 * ROW
VMEM = pl.BlockSpec(memory_space=pltpu.VMEM)
SMEM = pl.BlockSpec(memory_space=pltpu.SMEM)
HBM = pl.BlockSpec(memory_space=pltpu.HBM)
PEERS = (1, 3, 2)
STEPS = (0,) + PEERS
ARRIVAL = (0, 1, 3, 2)


def peer(index, s):
    return 3 - index if s == 3 else index ^ s


def pairs(move):
    found = []
    for i in range(256):
        x, h, c, z, y = i // 64, i // 16 % 4, i // 8 % 2, i // 4 % 2, i % 4
        x, h, c, z, y = move(x, h, c, z, y)
        found.append((i, ((x * 4 + h) * 2 + c) * 8 + z * 4 + y))
    return found


def far_plane(x, h, c, z, y):
    plane = (x * 8 + h * 2 + z + (1 if z else -1)) % 32
    return plane // 8, plane // 2 % 4, c, plane % 2, y


def straight(x, h, c, z, y):
    return x, h, z, c, y


def crossed_in(x, h, c, z, y):
    return x, h, 1 - z, c, y


def crossed_out(x, h, c, z, y):
    return x, h, z, 1 - c, y


def other_core(x, h, c, z, y):
    return x, h, 1 - c, z, y


def other_z(x, h, c, z, y):
    return x, h, c, 1 - z, y


def pair_h(x, h, c, z, y):
    return x, h ^ 1, c, z, y


def mirror_h(x, h, c, z, y):
    return x, 3 - h, c, z, y


def ring_z(x, h, c, z, y):
    return (x, (h + 1) % 4, c, 0, y) if z else (x, (h + 3) % 4, c, 1, y)


def pair_zh(x, h, c, z, y):
    return x, h ^ 1, c, 1 - z, y


def peer_x(s):
    return lambda x, h, c, z, y: (peer(x, s), h, c, z, y)


def peer_y(s):
    return lambda x, h, c, z, y: (x, h, c, z, peer(y, s))


def exchange(value, move):
    return lax.ppermute(value, ("depth", "filt"), pairs(move))


def shape(*dims, dtype=BF):
    return jax.ShapeDtypeStruct(dims, dtype)


def call(body, outs, scratch, *args, flops=0, moved=2_000_000, room=4, hbm_in=(), hbm_out=()):
    return pl.pallas_call(
        body,
        out_shape=outs,
        in_specs=[SMEM] + [HBM if i in hbm_in else VMEM for i in range(1, len(args))],
        out_specs=tuple(HBM if i in hbm_out else VMEM for i in range(len(outs))),
        scratch_shapes=scratch,
        compiler_params=pltpu.CompilerParams(vmem_limit_bytes=room * 1024 * 1024),
        cost_estimate=pl.CostEstimate(flops=flops, bytes_accessed=moved, transcendentals=0),
    )(*args)


def at(index, size):
    return pl.ds(pl.multiple_of(index * size, size), size)


Z, Y, C, X, INNER = range(5)


def shifted_columns(values, by):
    if by == 0:
        return values
    moved = pltpu.roll(values, (-by) % values.shape[1], 1)
    column = lax.broadcasted_iota(jnp.int32, values.shape, 1) % ROW
    inside = column < ROW - 1 if by > 0 else column > 0
    return jnp.where(inside, moved, jnp.zeros_like(moved))


def prepare_body(
    place, mine, partner, partner_rest, bias, early, late, middle, backward, biases, filters
):
    z, y, c = place[Z], place[Y], place[C]
    biases[at(z, 32), :] = jnp.broadcast_to(bias[...], (128, 32)).T
    thirds = partner[27].astype(F32)
    biases[at(1 - z, 32), :] = jnp.broadcast_to(
        (thirds[:, :1] + thirds[:, 1:2]) + thirds[:, 2:3], (32, 128)
    )
    for k in range(27):
        filters[k, at(z, 32), :] = mine[k]
        filters[k, at(1 - z, 32), at(c, 128)] = partner[k]
        filters[k, at(1 - z, 32), at(1 - c, 128)] = partner_rest[k]
    blocks = [(c + i) % 2 * 4 + peer(y, s) for s in ARRIVAL for i in range(2)]
    for k in range(0, 27, 2):
        two = filters[k : min(k + 2, 27)].reshape(-1, 256)
        lanes = slice(64 * k, 64 * k + two.shape[0])
        backward[:, lanes] = two.T
        by_arrival = jnp.concatenate([backward[at(block, 32), lanes] for block in blocks]).T
        for j in range(two.shape[0] // 64):
            a, b, d = (k + j) // 9, (k + j) // 3 % 3, (k + j) % 3
            if a == 1:
                middle[64 * d : 64 * d + 64, 256 * b : 256 * b + 256] = filters[k + j]
            else:
                rows, values = slice(128 * d + 32 * a, 128 * d + 32 * a + 64), by_arrival[64 * j : 64 * j + 64]
                early[rows, 192 * b : 192 * b + 192] = values[:, :192]
                late[rows, 64 * b : 64 * b + 64] = values[:, 192:]


def by_arrival(place, shards, window):
    c = place[C]
    n = window.shape[0]
    window[:, pl.ds(pl.multiple_of(GWIN * c, 128), 128)] = jnp.zeros((n, 128), BF)
    start = pl.ds(pl.multiple_of(128 * (1 - c), 128), GWIN)
    at_row = 0
    for shard in shards:
        window[at_row : at_row + shard.shape[0], start] = shard[...]
        at_row += shard.shape[0]


def gather_window(place, shards, window):
    y, c = place[Y], place[C]
    window[:, pl.ds(pl.multiple_of(GWIN * c, 128), 128)] = jnp.zeros((256, 128), BF)
    start = pl.ds(pl.multiple_of(128 * (1 - c), 128), GWIN)
    for n, part in enumerate(shards):
        block = (c + n % 2) % 2 * 4 + peer(y, ARRIVAL[n // 2])
        window[at(block, 32), start] = part[...]


def convolve(window, moved, weights, rows):
    def build(i, _):
        moved[at(i, 32), :] = window[at(i, 32), :][:, ROW : ROW + GWIN]
        return 0

    lax.fori_loop(0, window.shape[0] // 32, build, 0)
    for n in range(0, GWIN, 256):
        size = min(256, GWIN - n)
        planes = (window[:, n : n + size], moved[:, n : n + size], window[:, n + 128 : n + 128 + size])
        got = jnp.dot(weights[...], jnp.concatenate(planes), preferred_element_type=F32)
        left, right = shifted_columns(got[:rows], -1), shifted_columns(got[2 * rows :], 1)
        yield slice(n, n + size), left + got[rows : 2 * rows] + right


def early_body(place, *refs):
    shards, weights, part, window, moved = refs[:6], *refs[6:]
    by_arrival(place, shards, window)
    for cells, total in convolve(window, moved, weights, 128):
        part[:, cells] = total


def late_body(place, one, two, weights, part, near, far, window, moved):
    by_arrival(place, (one, two), window)
    lower = place[Z] == 0
    for cells, total in convolve(window, moved, weights, 128):
        total = total + part[:, cells]
        to_next, to_last = total[:64].astype(BF), total[64:].astype(BF)
        near[:, cells] = jnp.where(lower, to_next, to_last)
        far[:, cells] = jnp.where(lower, to_last, to_next)


def middle_body(place, *refs):
    shards, weights, mid, own, window, moved = refs[:8], *refs[8:]
    gather_window(place, shards, window)
    own[...] = window[:, 2 * ROW : 2 * ROW + OWN]
    for cells, total in convolve(window, moved, weights, 64):
        mid[:, cells] = total


def if_inner(place, values):
    return jnp.where(place[INNER] > 0, values, jnp.zeros_like(values))


def gelu_parts(place, mid, near, far, bias):
    v = mid[...] + bias[:, :1] + near[...].astype(F32) + if_inner(place, far[...].astype(F32))
    square = v * v
    t = jnp.tanh(0.7978845608028654 * (v + 0.044715 * (square * v)))
    return v, square, t


def grad_body(place, mid, near, far, bias, cot_own, cot_other, grad, sums, cot):
    c = place[C]
    cot[at(c, 32), :] = cot_own[...]
    cot[at(1 - c, 32), :] = cot_other[...]
    moved = pltpu.roll(cot[...].astype(F32), jnp.where(c == 0, ROW, GWIN - ROW), 1)
    cell = lax.broadcasted_iota(jnp.int32, moved.shape, 1)
    inside = (cell >= ROW * (1 - c)) & (cell < GWIN - ROW * c)
    cotangent = jnp.where(inside, moved, 0.0)
    v, square, t = gelu_parts(place, mid, near, far, bias)
    inner = 0.7978845608028654 * (1.0 + 3 * 0.044715 * square)
    slope = 0.5 * (1.0 + t) + 0.5 * v * (1.0 - t * t) * inner
    g = (cotangent * slope).astype(BF)
    grad[...] = g
    sums[...] = jnp.sum(g.astype(F32)[:, ROW : ROW + OWN], axis=1, keepdims=True)


def activated_body(place, mid, near, far, bias, mine, other, act):
    v, _, t = gelu_parts(place, mid, near, far, bias)
    act[...] = (v * (0.5 * (1.0 + t)))[:, ROW : ROW + OWN].astype(BF)
    mine[...] = act[at(place[C], 32), :]
    other[...] = act[at(1 - place[C], 32), :]


def shifted_grads(values, stack):
    values = values.astype(F32)
    for c in range(3):
        moved = shifted_columns(values, 1 - c).astype(BF)
        for b in range(3):
            k = (3 * b + c) * 64
            start = ROW * (2 - b)
            stack[k : k + 64, :] = moved[:, start : start + OWN]


def halves(values):
    high = values.astype(BF)
    low = (values - high.astype(F32)).astype(BF)
    lane = lax.broadcasted_iota(jnp.int32, values.shape, values.ndim - 1)
    return jnp.where(lane < 64, high, low)


def whole(values):
    values = values.astype(F32)
    return values + pltpu.roll(values, 64, values.ndim - 1)


def split(values, out):
    n = values.shape[0] * 27 // 28
    out[:n] = values[:n].astype(BF)
    out[n:] = halves(values[n:])


def join(ref):
    n = ref.shape[0] * 27 // 28
    return jnp.concatenate([ref[:n].astype(F32), whole(ref[n:])])


def kernel_grads(place, values, own, keep, send, stack):
    shifted_grads(values, stack)
    lower = place[C] == 0
    got = lax.dot_general(
        stack[...], own[...], (((1,), (1,)), ((), ())), preferred_element_type=F32
    )
    left, right = got[:, :128], got[:, 128:]
    keep[:18] = jnp.where(lower, left, right).reshape(18, 32, 128)
    send[:18] = jnp.where(lower, right, left).reshape(18, 32, 128).astype(BF)


def here_body(place, here, own, sums, keep, send, stack):
    kernel_grads(place, here[...], own, keep, send, stack)
    spread = jnp.broadcast_to(sums[...], (64, 128)).reshape(2, 32, 128)
    keep[18:] = spread
    send[18:] = halves(spread)


def near_body(place, near, own, keep, send, stack):
    kernel_grads(place, near[...], own, keep, send, stack)


def far_body(place, far, own, keep, send, stack):
    kernel_grads(place, if_inner(place, far[...]), own, keep, send, stack)


def input_grad_body(place, near, here, far, weights, *refs):
    outs, (stack, full) = refs[:4], refs[4:]
    lower = place[Z] == 0
    there, here, far = near[...], here[...], if_inner(place, far[...])
    shifted_grads(jnp.where(lower, there, far), stack.at[:576])
    shifted_grads(here, stack.at[576:1152])
    shifted_grads(jnp.where(lower, far, there), stack.at[1152:])
    for n in range(0, OWN, 256):
        full[:, n : n + 256] = jnp.dot(
            weights[...], stack[:, n : n + 256], preferred_element_type=F32
        ).astype(BF)
    y, c = place[Y], place[C]
    for s, out in zip(STEPS, outs, strict=True):
        for i in range(2):
            block = (c + i) % 2 * 4 + peer(y, s)
            out[32 * i : 32 * i + 32, :] = full[at(block, 32), :]


def fold_y_body(place, one, two, three, four, act_own, act_other, straight_out, crossed_out):
    total = (one[...].astype(F32) + four[...].astype(F32)) + (two[...].astype(F32) + three[...].astype(F32))
    total = total.astype(BF)
    straight_out[:32, :] = act_own[...]
    crossed_out[:32, :] = act_other[...]
    straight_out[32:, :] = total[:32]
    crossed_out[32:, :] = total[32:]


def place_body(place, direct, crossed, activated, input_grad):
    z = place[Z]
    for part, half in ((direct, z), (crossed, 1 - z)):
        activated[:, at(half, OWN)] = part[:32, :]
        input_grad[:, at(half, OWN)] = part[32:, :]


def fold_core_body(place, here, near, far, got_here, got_near, got_far, mine, *refs):
    outs, total = refs[:3], refs[3]
    x, z = place[X], place[Z]
    total[18:36] = here[:18] + got_here[:18].astype(F32)
    total[54:] = here[18:] + whole(got_here[18:])
    total[pl.ds(36 * z, 18)] = near[...] + got_near[...].astype(F32)
    total[pl.ds(36 * (1 - z), 18)] = far[...] + got_far[...].astype(F32)
    mine[...] = total[:, at(x, 8), :]
    for s, out in zip(PEERS, outs, strict=True):
        split(total[:, at(peer(x, s), 8), :], out)


def fold_x_body(place, mine, one, two, three, keep, send, total):
    total[...] = (mine[...] + join(one) + join(two) + join(three)).reshape(28, 2, 8, 128)
    split(total[:, pl.ds(place[Z], 1)].reshape(28, 8, 128), keep)
    split(total[:, pl.ds(1 - place[Z], 1)].reshape(28, 8, 128), send)


def fold_zh_body(place, mine, from_z, from_h, from_zh, out):
    split((join(mine) + join(from_z)) + (join(from_h) + join(from_zh)), out)


def fold_h_body(place, mine, got, out):
    split(join(mine) + join(got), out)


def quarters_body(place, *refs):
    parts, out, full = refs[:4], refs[4], refs[5]
    for s, part in zip(STEPS, parts, strict=True):
        full[:, at(peer(place[X], s), 8), :] = part[...].astype(F32)
    out[...] = full[...].astype(BF)


def whole_body(place, mine, other, taps, bias):
    taps[:, :, at(place[C], 128)] = mine[:27].astype(F32)
    taps[:, :, at(1 - place[C], 128)] = other[:27].astype(F32)
    bias[...] = whole(mine[27]).T[:1]


def local(volume, kernel, bias, cotangent):
    filt, depth = lax.axis_index("filt"), lax.axis_index("depth")
    z, c = filt // 4, depth % 2
    plane = depth // 2 * 2 + z
    inner = (plane > 0) & (plane < 31)
    place = jnp.stack([z, filt % 4, c, depth // 8, inner]).astype(jnp.int32)

    def halves_of(value):
        flat = value.reshape(32, 64 * ROW)
        first, second = flat[:, :GWIN], flat[:, 30 * ROW :]
        return jnp.where(z == 0, first, second), jnp.where(z == 0, second, first)

    direct, crossed = halves_of(volume)
    cot_direct, cot_crossed = halves_of(cotangent)

    direct, crossed = exchange(direct, straight), exchange(crossed, crossed_in)
    shards = [direct, crossed]
    shards += [exchange(shards[i], peer_y(s)) for s in PEERS[:2] for i in range(2)]
    last = [exchange(shards[4], peer_y(1)), exchange(shards[3], peer_y(3))]

    high = lax.reduce_precision(bias, 8, 7)
    middle = lax.reduce_precision(bias - high, 8, 7)
    lane = lax.broadcasted_iota(jnp.int32, (1, 32, 128), 2)
    parts = jnp.where(lane == 0, high[:, None], jnp.where(lane == 1, middle[:, None], (bias - high - middle)[:, None]))
    taps = lax.dynamic_slice(kernel, (0, 0, 128 * c), (27, 32, 128))
    taps = exchange(jnp.concatenate([taps, parts.astype(BF)]), ring_z)
    early_weights, late_weights, middle_weights, backward_weights, biases = call(
        prepare_body,
        (shape(384, 576), shape(384, 192), shape(192, 768), shape(256, 1728), shape(64, 128, dtype=F32)),
        [pltpu.VMEM((27, 64, 256), BF)],
        place,
        kernel,
        taps,
        exchange(taps, other_core),
        bias.reshape(1, 32),
        room=8,
    )
    cot_own, cot_other = exchange(cot_direct, straight), exchange(cot_crossed, crossed_in)

    def windows(channels):
        return [pltpu.VMEM((channels, VWIN), BF), pltpu.VMEM((channels, GWIN), BF)]

    (part,) = call(
        early_body,
        (shape(128, GWIN, dtype=F32),),
        windows(192),
        place,
        *shards,
        early_weights,
        flops=2 * 384 * 576 * GWIN,
        room=10,
    )
    near, far = call(
        late_body,
        (shape(64, GWIN), shape(64, GWIN)),
        windows(64),
        place,
        *last,
        late_weights,
        part,
        flops=2 * 384 * 192 * GWIN,
        room=10,
    )
    near, far = exchange(near, other_z), exchange(far, far_plane)
    mid, own = call(
        middle_body,
        (shape(64, GWIN, dtype=F32), shape(256, OWN)),
        windows(256),
        place,
        *shards,
        *last,
        middle_weights,
        flops=2 * 192 * 768 * GWIN,
        room=12,
    )
    grad, sums = call(
        grad_body,
        (shape(64, GWIN), shape(64, 1, dtype=F32)),
        [pltpu.VMEM((64, GWIN), BF)],
        place,
        mid,
        near,
        far,
        biases,
        cot_own,
        cot_other,
        room=12,
    )
    grad_near, grad_far = exchange(grad, other_z), exchange(grad, far_plane)
    act_own, act_other = call(
        activated_body,
        (shape(32, OWN), shape(32, OWN)),
        [pltpu.VMEM((64, OWN), BF)],
        place,
        mid,
        near,
        far,
        biases,
        room=12,
    )

    def wgrad(body, taps, *args):
        keep, send = call(
            body,
            (shape(taps, 32, 128, dtype=F32), shape(taps, 32, 128)),
            [pltpu.VMEM((9 * 64, OWN), BF)],
            place,
            *args,
            flops=2 * 576 * 256 * OWN,
            room=8,
        )
        return keep, exchange(send, other_core)

    grads = [
        wgrad(here_body, 20, grad, own, sums), wgrad(near_body, 18, grad_near, own), wgrad(far_body, 18, grad_far, own)
    ]
    pieces = call(
        input_grad_body,
        tuple(shape(64, OWN) for _ in STEPS),
        [pltpu.VMEM((27 * 64, OWN), BF), pltpu.VMEM((256, OWN), BF)],
        place,
        grad_near,
        grad,
        grad_far,
        backward_weights,
        flops=2 * 1728 * 256 * OWN,
        room=20,
    )

    parts = [pieces[0]] + [exchange(p, peer_y(s)) for s, p in zip(PEERS, pieces[1:])]
    direct, crossed = call(fold_y_body, (shape(64, OWN), shape(64, OWN)), [], place, *parts, act_own, act_other)
    activated, input_grad = call(
        place_body,
        (shape(32, 64 * ROW), shape(32, 64 * ROW)),
        [],
        place,
        exchange(direct, straight),
        exchange(crossed, crossed_out),
    )

    mine, *sends = call(
        fold_core_body,
        (shape(56, 8, 128, dtype=F32),) + (shape(56, 8, 128),) * 3,
        [pltpu.VMEM((56, 32, 128), F32)],
        place,
        *[keep for keep, _ in grads],
        *[got for _, got in grads],
    )
    got = [exchange(value, peer_x(s)) for s, value in zip(PEERS, sends)]
    eight = shape(28, 8, 128)
    keep, send = call(fold_x_body, (eight, eight), [pltpu.VMEM((28, 2, 8, 128), F32)], place, mine, *got)
    got = [exchange(send, other_z), exchange(keep, pair_h), exchange(send, pair_zh)]
    (part,) = call(fold_zh_body, (eight,), [], place, keep, *got)
    (part,) = call(fold_h_body, (eight,), [], place, part, exchange(part, mirror_h))
    got = [exchange(part, peer_x(s)) for s in PEERS]
    (part,) = call(quarters_body, (shape(28, 32, 128),), [pltpu.VMEM((28, 32, 128), F32)], place, part, *got)
    kernel_grad, bias_grad = call(
        whole_body,
        (shape(27, 32, 256, dtype=F32), shape(1, 32, dtype=F32)),
        [],
        place,
        part,
        exchange(part, other_core),
    )
    return (
        activated.reshape(32, 1, 64 * ROW),
        input_grad.reshape(32, 1, 64 * ROW),
        kernel_grad,
        bias_grad.reshape(32),
    )


def solution(mesh):
    placed = (P("filt", "depth", None), P(None, "filt", None), P("filt"), P("filt", "depth", None))
    return jax.shard_map(
        local,
        mesh=mesh,
        in_specs=placed,
        out_specs=(
            P("filt", "depth", None),
            P("filt", "depth", None),
            P(None, "filt", None),
            P("filt"),
        ),
        check_vma=False,
    )
```

```python
import jax
import jax.numpy as jnp
from jax import lax
from jax.experimental import pallas as pl
from jax.experimental.pallas import tpu as pltpu
from jax.sharding import PartitionSpec as P


BF = jnp.bfloat16
F32 = jnp.float32
ROW = 64
OWN = 32 * ROW
GWIN = 34 * ROW
VWIN = 36 * ROW
VMEM = pl.BlockSpec(memory_space=pltpu.VMEM)
SMEM = pl.BlockSpec(memory_space=pltpu.SMEM)
HBM = pl.BlockSpec(memory_space=pltpu.HBM)
PEERS = (1, 3, 2)
STEPS = (0,) + PEERS
ARRIVAL = (0, 1, 3, 2)


def peer(index, s):
    return 3 - index if s == 3 else index ^ s


def pairs(move):
    found = []
    for i in range(256):
        x, h, c, z, y = i // 64, i // 16 % 4, i // 8 % 2, i // 4 % 2, i % 4
        x, h, c, z, y = move(x, h, c, z, y)
        found.append((i, ((x * 4 + h) * 2 + c) * 8 + z * 4 + y))
    return found


def far_plane(x, h, c, z, y):
    plane = (x * 8 + h * 2 + z + (1 if z else -1)) % 32
    return plane // 8, plane // 2 % 4, c, plane % 2, y


def straight(x, h, c, z, y):
    return x, h, z, c, y


def crossed_in(x, h, c, z, y):
    return x, h, 1 - z, c, y


def crossed_out(x, h, c, z, y):
    return x, h, z, 1 - c, y


def other_core(x, h, c, z, y):
    return x, h, 1 - c, z, y


def other_z(x, h, c, z, y):
    return x, h, c, 1 - z, y


def pair_h(x, h, c, z, y):
    return x, h ^ 1, c, z, y


def mirror_h(x, h, c, z, y):
    return x, 3 - h, c, z, y


def ring_z(x, h, c, z, y):
    return (x, (h + 1) % 4, c, 0, y) if z else (x, (h + 3) % 4, c, 1, y)


def pair_zh(x, h, c, z, y):
    return x, h ^ 1, c, 1 - z, y


def peer_x(s):
    return lambda x, h, c, z, y: (peer(x, s), h, c, z, y)


def peer_y(s):
    return lambda x, h, c, z, y: (x, h, c, z, peer(y, s))


def exchange(value, move):
    return lax.ppermute(value, ("depth", "filt"), pairs(move))


def shape(*dims, dtype=BF):
    return jax.ShapeDtypeStruct(dims, dtype)


def call(body, outs, scratch, *args, flops=0, moved=2_000_000, room=4, hbm_in=(), hbm_out=()):
    return pl.pallas_call(
        body,
        out_shape=outs,
        in_specs=[SMEM] + [HBM if i in hbm_in else VMEM for i in range(1, len(args))],
        out_specs=tuple(HBM if i in hbm_out else VMEM for i in range(len(outs))),
        scratch_shapes=scratch,
        compiler_params=pltpu.CompilerParams(vmem_limit_bytes=room * 1024 * 1024),
        cost_estimate=pl.CostEstimate(flops=flops, bytes_accessed=moved, transcendentals=0),
    )(*args)


def at(index, size):
    return pl.ds(pl.multiple_of(index * size, size), size)


Z, Y, C, X, INNER = range(5)


def shifted_columns(values, by):
    if by == 0:
        return values
    moved = pltpu.roll(values, (-by) % values.shape[1], 1)
    column = lax.broadcasted_iota(jnp.int32, values.shape, 1) % ROW
    inside = column < ROW - 1 if by > 0 else column > 0
    return jnp.where(inside, moved, jnp.zeros_like(moved))


def prepare_body(
    place, mine, partner, partner_rest, bias, early, late, middle, backward, biases, filters
):
    z, y, c = place[Z], place[Y], place[C]
    biases[at(z, 32), :] = jnp.broadcast_to(bias[...], (128, 32)).T
    thirds = partner[27].astype(F32)
    biases[at(1 - z, 32), :] = jnp.broadcast_to(
        (thirds[:, :1] + thirds[:, 1:2]) + thirds[:, 2:3], (32, 128)
    )
    for k in range(27):
        filters[k, at(z, 32), :] = mine[k]
        filters[k, at(1 - z, 32), at(c, 128)] = partner[k]
        filters[k, at(1 - z, 32), at(1 - c, 128)] = partner_rest[k]
    blocks = [(c + i) % 2 * 4 + peer(y, s) for s in ARRIVAL for i in range(2)]
    for k in range(0, 27, 2):
        two = filters[k : min(k + 2, 27)].reshape(-1, 256)
        lanes = slice(64 * k, 64 * k + two.shape[0])
        backward[:, lanes] = two.T
        by_arrival = jnp.concatenate([backward[at(block, 32), lanes] for block in blocks]).T
        for j in range(two.shape[0] // 64):
            a, b, d = (k + j) // 9, (k + j) // 3 % 3, (k + j) % 3
            if a == 1:
                middle[64 * d : 64 * d + 64, 256 * b : 256 * b + 256] = filters[k + j]
            else:
                rows, values = slice(128 * d + 32 * a, 128 * d + 32 * a + 64), by_arrival[64 * j : 64 * j + 64]
                early[rows, 192 * b : 192 * b + 192] = values[:, :192]
                late[rows, 64 * b : 64 * b + 64] = values[:, 192:]


def by_arrival(place, shards, window):
    c = place[C]
    n = window.shape[0]
    window[:, pl.ds(pl.multiple_of(GWIN * c, 128), 128)] = jnp.zeros((n, 128), BF)
    start = pl.ds(pl.multiple_of(128 * (1 - c), 128), GWIN)
    at_row = 0
    for shard in shards:
        window[at_row : at_row + shard.shape[0], start] = shard[...]
        at_row += shard.shape[0]


def gather_window(place, shards, window):
    y, c = place[Y], place[C]
    window[:, pl.ds(pl.multiple_of(GWIN * c, 128), 128)] = jnp.zeros((256, 128), BF)
    start = pl.ds(pl.multiple_of(128 * (1 - c), 128), GWIN)
    for n, part in enumerate(shards):
        block = (c + n % 2) % 2 * 4 + peer(y, ARRIVAL[n // 2])
        window[at(block, 32), start] = part[...]


def convolve(window, moved, weights, rows):
    def build(i, _):
        moved[at(i, 32), :] = window[at(i, 32), :][:, ROW : ROW + GWIN]
        return 0

    lax.fori_loop(0, window.shape[0] // 32, build, 0)
    for n in range(0, GWIN, 256):
        size = min(256, GWIN - n)
        planes = (window[:, n : n + size], moved[:, n : n + size], window[:, n + 128 : n + 128 + size])
        got = jnp.dot(weights[...], jnp.concatenate(planes), preferred_element_type=F32)
        left, right = shifted_columns(got[:rows], -1), shifted_columns(got[2 * rows :], 1)
        yield slice(n, n + size), left + got[rows : 2 * rows] + right


def early_body(place, *refs):
    shards, weights, part, window, moved = refs[:6], *refs[6:]
    by_arrival(place, shards, window)
    for cells, total in convolve(window, moved, weights, 128):
        part[:, cells] = total


def late_body(place, one, two, weights, part, near, far, window, moved):
    by_arrival(place, (one, two), window)
    lower = place[Z] == 0
    for cells, total in convolve(window, moved, weights, 128):
        total = total + part[:, cells]
        to_next, to_last = total[:64].astype(BF), total[64:].astype(BF)
        near[:, cells] = jnp.where(lower, to_next, to_last)
        far[:, cells] = jnp.where(lower, to_last, to_next)


def middle_body(place, *refs):
    shards, weights, cot_own, cot_other, mid, own, cotangent, window, moved, cot = refs[:8], *refs[8:]
    gather_window(place, shards, window)
    own[...] = window[:, 2 * ROW : 2 * ROW + OWN]
    for cells, total in convolve(window, moved, weights, 64):
        mid[:, cells] = total
    c = place[C]
    cot[at(c, 32), :] = cot_own[...]
    cot[at(1 - c, 32), :] = cot_other[...]
    shift = pltpu.roll(cot[...].astype(F32), jnp.where(c == 0, ROW, GWIN - ROW), 1)
    cell = lax.broadcasted_iota(jnp.int32, shift.shape, 1)
    inside = (cell >= ROW * (1 - c)) & (cell < GWIN - ROW * c)
    cotangent[...] = jnp.where(inside, shift, 0.0)


def if_inner(place, values):
    return jnp.where(place[INNER] > 0, values, jnp.zeros_like(values))


def gelu_parts(place, mid, near, far, bias):
    v = mid[...] + bias[:, :1] + near[...].astype(F32) + if_inner(place, far[...].astype(F32))
    square = v * v
    t = jnp.tanh(0.7978845608028654 * (v + 0.044715 * (square * v)))
    return v, square, t


def grad_body(place, mid, near, far, bias, cotangent, grad, sums):
    v, square, t = gelu_parts(place, mid, near, far, bias)
    inner = 0.7978845608028654 * (1.0 + 3 * 0.044715 * square)
    slope = 0.5 * (1.0 + t) + 0.5 * v * (1.0 - t * t) * inner
    g = (cotangent[...] * slope).astype(BF)
    grad[...] = g
    sums[...] = jnp.sum(g.astype(F32)[:, ROW : ROW + OWN], axis=1, keepdims=True)


def activated_body(place, mid, near, far, bias, mine, other, act):
    v, _, t = gelu_parts(place, mid, near, far, bias)
    act[...] = (v * (0.5 * (1.0 + t)))[:, ROW : ROW + OWN].astype(BF)
    mine[...] = act[at(place[C], 32), :]
    other[...] = act[at(1 - place[C], 32), :]


def shifted_grads(values, stack):
    values = values.astype(F32)
    for c in range(3):
        moved = shifted_columns(values, 1 - c).astype(BF)
        for b in range(3):
            k = (3 * b + c) * 64
            start = ROW * (2 - b)
            stack[k : k + 64, :] = moved[:, start : start + OWN]


def halves(values):
    high = values.astype(BF)
    low = (values - high.astype(F32)).astype(BF)
    lane = lax.broadcasted_iota(jnp.int32, values.shape, values.ndim - 1)
    return jnp.where(lane < 64, high, low)


def whole(values):
    values = values.astype(F32)
    return values + pltpu.roll(values, 64, values.ndim - 1)


def split(values, out):
    n = values.shape[0] * 27 // 28
    out[:n] = values[:n].astype(BF)
    out[n:] = halves(values[n:])


def join(ref):
    n = ref.shape[0] * 27 // 28
    return jnp.concatenate([ref[:n].astype(F32), whole(ref[n:])])


def kernel_grads(place, values, own, keep, send, stack):
    shifted_grads(values, stack)
    lower = place[C] == 0
    got = lax.dot_general(
        stack[...], own[...], (((1,), (1,)), ((), ())), preferred_element_type=F32
    )
    left, right = got[:, :128], got[:, 128:]
    keep[:18] = jnp.where(lower, left, right).reshape(18, 32, 128)
    send[:18] = jnp.where(lower, right, left).reshape(18, 32, 128).astype(BF)


def here_body(place, here, own, sums, keep, send, stack):
    kernel_grads(place, here[...], own, keep, send, stack)
    spread = jnp.broadcast_to(sums[...], (64, 128)).reshape(2, 32, 128)
    keep[18:] = spread
    send[18:] = halves(spread)


def near_body(place, near, own, here_keep, here_send, keep, send, stack):
    kernel_grads(place, near[...], own, keep, send, stack)
    keep[18:] = here_keep[...]
    send[18:] = here_send[...]


def far_body(place, far, own, keep, send, stack):
    kernel_grads(place, if_inner(place, far[...]), own, keep, send, stack)


def input_grad_body(place, near, here, far, weights, *refs):
    outs, (stack, full) = refs[:4], refs[4:]
    lower = place[Z] == 0
    there, here, far = near[...], here[...], if_inner(place, far[...])
    shifted_grads(jnp.where(lower, there, far), stack.at[:576])
    shifted_grads(here, stack.at[576:1152])
    shifted_grads(jnp.where(lower, far, there), stack.at[1152:])
    for n in range(0, OWN, 256):
        full[:, n : n + 256] = jnp.dot(
            weights[...], stack[:, n : n + 256], preferred_element_type=F32
        ).astype(BF)
    y, c = place[Y], place[C]
    for s, out in zip(STEPS, outs, strict=True):
        for i in range(2):
            block = (c + i) % 2 * 4 + peer(y, s)
            out[32 * i : 32 * i + 32, :] = full[at(block, 32), :]


def fold_y_body(place, one, two, three, four, act_own, act_other, straight_out, crossed_out):
    total = (one[...].astype(F32) + four[...].astype(F32)) + (two[...].astype(F32) + three[...].astype(F32))
    total = total.astype(BF)
    straight_out[:32, :] = act_own[...]
    crossed_out[:32, :] = act_other[...]
    straight_out[32:, :] = total[:32]
    crossed_out[32:, :] = total[32:]


def place_body(place, direct, crossed, activated, input_grad):
    z = place[Z]
    for part, half in ((direct, z), (crossed, 1 - z)):
        activated[:, at(half, OWN)] = part[:32, :]
        input_grad[:, at(half, OWN)] = part[32:, :]


def fold_core_body(place, near, far, got_near, got_far, mine, *refs):
    outs, total = refs[:3], refs[3]
    x, z = place[X], place[Z]
    total[18:36] = near[18:36] + got_near[18:36].astype(F32)
    total[54:] = near[36:] + whole(got_near[36:])
    total[pl.ds(36 * z, 18)] = near[:18] + got_near[:18].astype(F32)
    total[pl.ds(36 * (1 - z), 18)] = far[...] + got_far[...].astype(F32)
    mine[...] = total[:, at(x, 8), :]
    for s, out in zip(PEERS, outs, strict=True):
        split(total[:, at(peer(x, s), 8), :], out)


def fold_x_body(place, mine, one, two, three, keep, send, total):
    total[...] = (mine[...] + join(one) + join(two) + join(three)).reshape(28, 2, 8, 128)
    split(total[:, pl.ds(place[Z], 1)].reshape(28, 8, 128), keep)
    split(total[:, pl.ds(1 - place[Z], 1)].reshape(28, 8, 128), send)


def fold_zh_body(place, mine, from_z, from_h, from_zh, out):
    split((join(mine) + join(from_z)) + (join(from_h) + join(from_zh)), out)


def fold_h_body(place, mine, got, out):
    split(join(mine) + join(got), out)


def quarters_body(place, *refs):
    parts, out, full = refs[:4], refs[4], refs[5]
    for s, part in zip(STEPS, parts, strict=True):
        full[:, at(peer(place[X], s), 8), :] = part[...].astype(F32)
    out[...] = full[...].astype(BF)


def whole_body(place, mine, other, taps, bias):
    taps[:, :, at(place[C], 128)] = mine[:27].astype(F32)
    taps[:, :, at(1 - place[C], 128)] = other[:27].astype(F32)
    bias[...] = whole(mine[27]).T[:1]


def local(volume, kernel, bias, cotangent):
    filt, depth = lax.axis_index("filt"), lax.axis_index("depth")
    z, c = filt // 4, depth % 2
    plane = depth // 2 * 2 + z
    inner = (plane > 0) & (plane < 31)
    place = jnp.stack([z, filt % 4, c, depth // 8, inner]).astype(jnp.int32)

    def halves_of(value):
        flat = value.reshape(32, 64 * ROW)
        first, second = flat[:, :GWIN], flat[:, 30 * ROW :]
        return jnp.where(z == 0, first, second), jnp.where(z == 0, second, first)

    direct, crossed = halves_of(volume)
    cot_direct, cot_crossed = halves_of(cotangent)

    direct, crossed = exchange(direct, straight), exchange(crossed, crossed_in)
    shards = [direct, crossed]
    shards += [exchange(shards[i], peer_y(s)) for s in PEERS[:2] for i in range(2)]
    last = [exchange(shards[4], peer_y(1)), exchange(shards[3], peer_y(3))]

    high = lax.reduce_precision(bias, 8, 7)
    middle = lax.reduce_precision(bias - high, 8, 7)
    lane = lax.broadcasted_iota(jnp.int32, (1, 32, 128), 2)
    parts = jnp.where(lane == 0, high[:, None], jnp.where(lane == 1, middle[:, None], (bias - high - middle)[:, None]))
    taps = lax.dynamic_slice(kernel, (0, 0, 128 * c), (27, 32, 128))
    taps = exchange(jnp.concatenate([taps, parts.astype(BF)]), ring_z)
    early_weights, late_weights, middle_weights, backward_weights, biases = call(
        prepare_body,
        (shape(384, 576), shape(384, 192), shape(192, 768), shape(256, 1728), shape(64, 128, dtype=F32)),
        [pltpu.VMEM((27, 64, 256), BF)],
        place,
        kernel,
        taps,
        exchange(taps, other_core),
        bias.reshape(1, 32),
        room=8,
    )
    cot_own, cot_other = exchange(cot_direct, straight), exchange(cot_crossed, crossed_in)

    def windows(channels):
        return [pltpu.VMEM((channels, VWIN), BF), pltpu.VMEM((channels, GWIN), BF)]

    (part,) = call(
        early_body,
        (shape(128, GWIN, dtype=F32),),
        windows(192),
        place,
        *shards,
        early_weights,
        flops=2 * 384 * 576 * GWIN,
        room=10,
    )
    near, far = call(
        late_body,
        (shape(64, GWIN), shape(64, GWIN)),
        windows(64),
        place,
        *last,
        late_weights,
        part,
        flops=2 * 384 * 192 * GWIN,
        room=10,
    )
    near, far = exchange(near, other_z), exchange(far, far_plane)
    mid, own, cotangent = call(
        middle_body,
        (shape(64, GWIN, dtype=F32), shape(256, OWN), shape(64, GWIN, dtype=F32)),
        windows(256) + [pltpu.VMEM((64, GWIN), BF)],
        place,
        *shards,
        *last,
        middle_weights,
        cot_own,
        cot_other,
        flops=2 * 192 * 768 * GWIN,
        room=12,
    )
    grad, sums = call(
        grad_body, (shape(64, GWIN), shape(64, 1, dtype=F32)), [], place, mid, near, far, biases, cotangent, room=12
    )
    grad_near, grad_far = exchange(grad, other_z), exchange(grad, far_plane)
    act_own, act_other = call(
        activated_body,
        (shape(32, OWN), shape(32, OWN)),
        [pltpu.VMEM((64, OWN), BF)],
        place,
        mid,
        near,
        far,
        biases,
        room=12,
    )

    def wgrad(body, taps, *args):
        keep, send = call(
            body,
            (shape(taps, 32, 128, dtype=F32), shape(taps, 32, 128)),
            [pltpu.VMEM((9 * 64, OWN), BF)],
            place,
            *args,
            flops=2 * 576 * 256 * OWN,
            room=8,
        )
        return keep, send

    grads = wgrad(here_body, 20, grad, own, sums)
    keeps, sends = zip(wgrad(near_body, 38, grad_near, own, *grads), wgrad(far_body, 18, grad_far, own))
    pieces = call(
        input_grad_body,
        tuple(shape(64, OWN) for _ in STEPS),
        [pltpu.VMEM((27 * 64, OWN), BF), pltpu.VMEM((256, OWN), BF)],
        place,
        grad_near,
        grad,
        grad_far,
        backward_weights,
        flops=2 * 1728 * 256 * OWN,
        room=20,
    )

    parts = [pieces[0]] + [exchange(p, peer_y(s)) for s, p in zip(PEERS, pieces[1:])]
    direct, crossed = call(fold_y_body, (shape(64, OWN), shape(64, OWN)), [], place, *parts, act_own, act_other)
    activated, input_grad = call(
        place_body,
        (shape(32, 64 * ROW), shape(32, 64 * ROW)),
        [],
        place,
        exchange(direct, straight),
        exchange(crossed, crossed_out),
    )

    mine, *sends = call(
        fold_core_body,
        (shape(56, 8, 128, dtype=F32),) + (shape(56, 8, 128),) * 3,
        [pltpu.VMEM((56, 32, 128), F32)],
        place,
        *keeps,
        exchange(sends[0], other_core),
        exchange(sends[1], other_core),
    )
    got = [exchange(value, peer_x(s)) for s, value in zip(PEERS, sends)]
    eight = shape(28, 8, 128)
    keep, send = call(fold_x_body, (eight, eight), [pltpu.VMEM((28, 2, 8, 128), F32)], place, mine, *got)
    got = [exchange(send, other_z), exchange(keep, pair_h), exchange(send, pair_zh)]
    (part,) = call(fold_zh_body, (eight,), [], place, keep, *got)
    (part,) = call(fold_h_body, (eight,), [], place, part, exchange(part, mirror_h))
    got = [exchange(part, peer_x(s)) for s in PEERS]
    (part,) = call(quarters_body, (shape(28, 32, 128),), [pltpu.VMEM((28, 32, 128), F32)], place, part, *got)
    kernel_grad, bias_grad = call(
        whole_body,
        (shape(27, 32, 256, dtype=F32), shape(1, 32, dtype=F32)),
        [],
        place,
        part,
        exchange(part, other_core),
    )
    return (
        activated.reshape(32, 1, 64 * ROW),
        input_grad.reshape(32, 1, 64 * ROW),
        kernel_grad,
        bias_grad.reshape(32),
    )


def solution(mesh):
    placed = (P("filt", "depth", None), P(None, "filt", None), P("filt"), P("filt", "depth", None))
    return jax.shard_map(
        local,
        mesh=mesh,
        in_specs=placed,
        out_specs=(
            P("filt", "depth", None),
            P("filt", "depth", None),
            P(None, "filt", None),
            P("filt"),
        ),
        check_vma=False,
    )
```
